32 devices in a mesh: seq: 4 (over z), head: 2 (over core), dp: 4 (over y, x).
Axes of the slice: x: 2, y: 2, z: 4, core: 2. Of those that a mesh axis runs over, the one named last changes fastest.
Arguments:
- hidden: bfloat16 [4, 768, 1024], P('dp', 'seq'), may hold values from -6 to 6
- norm_gain: float32 [1024], replicated, may hold values from 0.5 to 1.5
- projection: bfloat16 [3, 1024, 1024], P(None, None, 'head'), may hold values from -1 to 1
- upstream: bfloat16 [4, 768, 1024], P('dp', 'seq', 'head'), may hold values from -6 to 6
- cluster: int32 [4, 768, 1], P('dp', 'seq'), may hold values from 0 to 3; in each aligned block of 192 rows (0 to 191, 192 to 383, ..., all dimensions but the last counted through in order) at most 144 rows name the same one
Outputs:
- input_gradient: bfloat16 [4, 768, 1024], P('dp', 'seq', 'head')
- gain_gradient: float32 [1024], P('head')
The draws below stay inside these ranges and needn't reach their ends.
Inputs may be any that keep to these rules, and one draw needn't show every extreme that they name: Among the 192 tokens of one device no cluster is named more than 144 times, a bound that some block reaches.
All inputs are finite; a program needn't handle non-finite values.
Results may differ from the reference program's by a relative error of at most 0.01.
The reference program's roundings to bfloat16 on the way count: a program that leaves them out, or rounds other values in their place, can miss the bound.
Values may be sent and summed in bfloat16 or wider, within the bound.
A program may use at most 64 MiB of HBM per device.

```python
import math
import jax
import jax.numpy as jnp
import numpy as np
from jax import lax

D = 1024
HDIM = 64
TOK_DEV = 192
CLUSTERS = 4
HE = 1024
GROUP_HEADS = 8
LEN = 768
SEQS = 4
SLOT = 144
ROWS = 576
N_HEAD = 2


def draw_hidden(key, part):
    samples = jax.random.normal(jax.random.fold_in(key, 1), (SEQS, LEN, D), jnp.float32)
    return jnp.clip(samples, -6.0, 6.0).astype(jnp.bfloat16)


def draw_projection(key, part):
    weights_base = jax.random.normal(jax.random.fold_in(key, 11), (3, D, HE), jnp.float32) / math.sqrt(D)
    return jnp.clip(weights_base, -1.0, 1.0).astype(jnp.bfloat16)


def levels(stream_key, shape, shards, low, top_value):
    def one(axis_at, blocks):
        steps = jax.random.uniform(jax.random.fold_in(jax.random.fold_in(stream_key, 6), axis_at), (blocks,), jnp.float32, low / len(shards), top_value / len(shards))
        return jnp.repeat(jnp.exp(steps), shape[axis_at] // blocks).reshape((-1,) + (1,) * (len(shape) - axis_at - 1))

    loudness = one(*shards[0])
    for cut in shards[1:]:
        loudness = loudness * one(*cut)
    return loudness


def deal_out(stream_key, own, number, rows, count, top, reach, skew):
    ranking = jax.random.permutation(stream_key, count)
    heavy_load, ordinary = portions_of(count, rows * top, reach, skew, True), portions_of(count, rows * top, reach, skew, False)
    places = jnp.arange(count)

    def named(lengths, offset_by):
        used = int((lengths > 0).sum())
        fixed = max(1, used // 4)
        passed = fixed + (places - fixed + offset_by * (used - fixed)) % max(1, count - fixed)
        return jnp.zeros((count,), jnp.int32).at[ranking[jnp.where(places < fixed, places, passed)]].set(jnp.asarray(lengths, jnp.int32))

    lengths = jnp.where(number % 4 == 0, named(heavy_load, number // 4), named(ordinary, number - number // 4 - 1))
    mixed = jax.random.permutation(jax.random.fold_in(own, 3), count)
    source_of, taker = mixed[0:count // 2 * 2:2], mixed[1:count // 2 * 2:2]
    room = jnp.minimum(lengths[source_of] - 1, reach - lengths[taker]) // 2
    room = jnp.where((source_of == ranking[0]) | (taker == ranking[0]) | (lengths[taker] == 0), 0, jnp.maximum(room, 0))
    passed = jax.random.randint(jax.random.fold_in(own, 4), (count // 2,), 0, 1 << 20) % (room + 1)
    lengths = lengths.at[source_of].add(-passed).at[taker].add(passed)
    items = jnp.searchsorted(jnp.cumsum(lengths), jnp.arange(rows * top), side="right").astype(jnp.int32)
    listing = items.reshape(top, rows).T
    listing = listing[jax.random.permutation(jax.random.fold_in(own, 1), rows)]
    offset_by = jax.random.randint(jax.random.fold_in(own, 2), (rows, 1), 0, top)
    return jnp.take_along_axis(listing, (jnp.arange(top)[None, :] + offset_by) % top, axis=1)


def portions_of(number_of, total, bound, skew, full):
    loads = [(1 << 20) // math.isqrt(grade ** skew) + 1 for grade in range(1, number_of + 1)]
    largest = bound if full else min(bound, max(-(-total // number_of), total * loads[0] // sum(loads)))
    least = 1 if total - largest >= number_of - 1 else 0
    given, spare = [largest] + [least] * (number_of - 1), total - largest - least * (number_of - 1)
    while spare > 0:
        free = [i for i in range(1, number_of) if given[i] < largest] or [i for i in range(1, number_of) if given[i] < bound]
        whole, left = sum([loads[i] for i in free]), spare
        for i in free:
            extra = min(bound - given[i], max(1, left * loads[i] // whole), spare)
            given[i] = given[i] + extra
            spare = spare - extra
    return np.array(given)


def gaussian(own_key, shape, deviation, most, split=(), held_as=jnp.bfloat16):
    drawn = deviation * jax.random.normal(own_key, shape, jnp.float32)
    if split:
        drawn = drawn * levels(own_key, shape, split, -0.22, 0.18)
    return jnp.clip(drawn, -most, most).astype(held_as)


def setup_inputs(seed: int = 0) -> dict:
    splits = jax.random.split(jax.random.key(seed), 6)
    hidden = draw_hidden(jax.random.fold_in(splits[5], 71), 0)
    norm_gain = jnp.clip(1.0 + 0.1 * jax.random.normal(splits[1], (D,), jnp.float32), 0.5, 1.5)
    projection = draw_projection(jax.random.fold_in(splits[5], 71), 0)
    upstream = gaussian(splits[3], (SEQS, LEN, HE), 1.0, 6.0, ((0, 4), (1, 4), (2, 2)))
    cluster_keys = jax.random.split(jax.random.fold_in(splits[4], 1), SEQS * LEN // TOK_DEV)
    cluster_turns = jax.random.permutation(jax.random.fold_in(splits[4], 3), SEQS * LEN // TOK_DEV)
    cluster = jax.vmap(lambda own, number: deal_out(jax.random.fold_in(splits[4], 2), own, number, TOK_DEV, CLUSTERS, 1, SLOT, 2))(cluster_keys, cluster_turns).reshape((SEQS, LEN, 1))
    return dict(hidden=hidden, norm_gain=norm_gain, projection=projection, upstream=upstream, cluster=cluster)


epsilon = 1e-05
masked = -1e+30

def normalize(values, norm_gain):
    values = values.astype(jnp.float32)
    center = values - lax.optimization_barrier(jnp.mean(values, -1, keepdims=True))
    spread = lax.rsqrt(lax.optimization_barrier(jnp.mean(center * center, -1, keepdims=True)) + epsilon)
    scaled = center * spread
    return (scaled, spread, (scaled * norm_gain).astype(jnp.bfloat16))

def attend_backward(queries, key_rows, values, upstream, allowed, factor):
    scores = lax.dot_general(queries, key_rows, (((1,), (1,)), ((), ())), preferred_element_type=jnp.float32) * factor
    scores = jnp.where(allowed, scores, masked)
    powers = jnp.exp(scores - lax.optimization_barrier(jnp.max(scores, -1, keepdims=True)))
    weights = powers / lax.optimization_barrier(jnp.sum(powers, -1, keepdims=True))
    rounded = weights.astype(jnp.bfloat16)
    output = jnp.dot(rounded, values, preferred_element_type=jnp.float32)
    center_term = lax.optimization_barrier(jnp.sum(upstream.astype(jnp.float32) * output, -1, keepdims=True))
    grad_values = lax.dot_general(rounded, upstream, (((0,), (0,)), ((), ())), preferred_element_type=jnp.float32).astype(jnp.bfloat16)
    grad_weights = lax.dot_general(upstream, values, (((1,), (1,)), ((), ())), preferred_element_type=jnp.float32)
    grad_scores = (weights * (grad_weights - center_term) * factor).astype(jnp.bfloat16)
    grad_queries = jnp.dot(grad_scores, key_rows, preferred_element_type=jnp.float32).astype(jnp.bfloat16)
    grad_keys = lax.dot_general(grad_scores, queries, (((0,), (0,)), ((), ())), preferred_element_type=jnp.float32).astype(jnp.bfloat16)
    return (grad_queries, grad_keys, grad_values)

def cluster_grads(payload, validity, head_width):
    row_count = payload.shape[0]
    spans = payload.shape[1] // 4
    heads_local = spans // head_width
    positions = lax.broadcasted_iota(jnp.int32, (row_count, row_count), 0)
    others = lax.broadcasted_iota(jnp.int32, (row_count, row_count), 1)
    allowed = (positions >= others) & (validity[None, :] > 0)
    factor = head_width ** (-0.5)

    def one_head(head_index, result):
        offset = head_index * head_width

        def select(portion):
            return lax.dynamic_slice_in_dim(payload, portion * spans + offset, head_width, 1)
        grads_head = attend_backward(select(0), select(1), select(2), select(3), allowed, factor)
        for portion in range(3):
            result = lax.dynamic_update_slice_in_dim(result, grads_head[portion], portion * spans + offset, 1)
        return result
    return lax.fori_loop(0, heads_local, one_head, jnp.zeros((row_count, 3 * spans), jnp.bfloat16))

def reference(hidden, norm_gain, projection, upstream, cluster):
    scaled, spread, normed = normalize(hidden, norm_gain)
    flattened = normed.reshape(-1, D)
    projected = [jnp.dot(flattened, projection[portion], preferred_element_type=jnp.float32).astype(jnp.bfloat16).reshape(SEQS, LEN, HE) for portion in range(3)]
    group_width = GROUP_HEADS * HDIM
    gradients = []
    for sequence in range(SEQS):
        labels = cluster[sequence, :, 0]
        member = (labels[:, None] == jnp.arange(CLUSTERS, dtype=jnp.int32)[None, :]).astype(jnp.int32)
        counts = lax.optimization_barrier(jnp.sum(member, 0)).astype(jnp.int32)
        ordering = jnp.argsort(labels, stable=True).astype(jnp.int32)
        starts = (jnp.cumsum(counts) - counts).astype(jnp.int32)
        within = jnp.arange(ROWS, dtype=jnp.int32)
        validity = within[None, :] < counts[:, None]
        source_rows = jnp.where(validity, ordering[jnp.minimum(starts[:, None] + within[None, :], LEN - 1)], LEN).astype(jnp.int32)
        payload = jnp.concatenate([projected[0][sequence], projected[1][sequence], projected[2][sequence], upstream[sequence]], 1)
        padded = jnp.concatenate([payload, jnp.zeros((1, 4 * HE), jnp.bfloat16)], 0)

        def per_cluster(entries):
            return cluster_grads(padded[entries[0]], entries[1].astype(jnp.float32), HDIM)
        cluster_out = lax.map(per_cluster, (source_rows, validity))
        restored = jnp.zeros((LEN + 1, 3 * HE), jnp.bfloat16).at[source_rows.reshape(-1)].set(cluster_out.reshape(-1, 3 * HE))[:LEN]
        partial_value = jnp.zeros((LEN, D), jnp.float32)
        for group_index in range(N_HEAD):
            column_start = group_index * group_width
            group_term = jnp.zeros((LEN, D), jnp.float32)
            for portion in range(3):
                first = portion * HE + column_start
                group_term = group_term + jnp.dot(restored[:, first:first + group_width], projection[portion][:, column_start:column_start + group_width].T, preferred_element_type=jnp.float32)
            partial_value = partial_value + lax.optimization_barrier(group_term.astype(jnp.bfloat16)).astype(jnp.float32)
        gradients.append(partial_value)
    grad_normed = jnp.stack(gradients, 0)
    gain_gradient = lax.optimization_barrier(jnp.sum(grad_normed * scaled, (0, 1))) * (SEQS * LEN) ** (-0.5)
    grad_scaled = grad_normed * norm_gain
    first_mean = lax.optimization_barrier(jnp.mean(grad_scaled, -1, keepdims=True))
    second_mean = lax.optimization_barrier(jnp.mean(grad_scaled * scaled, -1, keepdims=True))
    input_gradient = (spread * (grad_scaled - first_mean - scaled * second_mean)).astype(jnp.bfloat16)
    return (input_gradient, gain_gradient)
```

```python
import functools

import jax
import jax.numpy as jnp
from jax import lax
from jax.experimental import pallas as pl
from jax.experimental.pallas import tpu as pltpu
from jax.sharding import PartitionSpec as P

HDIM = 64
CLUS_DEV = 1


epsilon = 1e-05
masked = -1e30


def normalize(values, norm_gain):
    values = values.astype(jnp.float32)
    center = values - jnp.mean(values, -1, keepdims=True)
    spread = lax.rsqrt(jnp.mean(center * center, -1, keepdims=True) + epsilon)
    scaled = center * spread
    return (scaled, spread, (scaled * norm_gain).astype(jnp.bfloat16))


def attend_backward(queries, key_rows, values, upstream, allowed, factor):
    scores = (
        lax.dot_general(
            queries, key_rows, (((1,), (1,)), ((), ())), preferred_element_type=jnp.float32
        )
        * factor
    )
    scores = jnp.where(allowed, scores, masked)
    powers = jnp.exp(scores - jnp.max(scores, -1, keepdims=True))
    weights = powers / jnp.sum(powers, -1, keepdims=True)
    rounded = weights.astype(jnp.bfloat16)
    output = jnp.dot(rounded, values, preferred_element_type=jnp.float32)
    center_term = jnp.sum(upstream.astype(jnp.float32) * output, -1, keepdims=True)
    grad_values = lax.dot_general(
        rounded, upstream, (((0,), (0,)), ((), ())), preferred_element_type=jnp.float32
    ).astype(jnp.bfloat16)
    grad_weights = lax.dot_general(
        upstream, values, (((1,), (1,)), ((), ())), preferred_element_type=jnp.float32
    )
    grad_scores = (weights * (grad_weights - center_term) * factor).astype(jnp.bfloat16)
    grad_queries = jnp.dot(grad_scores, key_rows, preferred_element_type=jnp.float32).astype(
        jnp.bfloat16
    )
    grad_keys = lax.dot_general(
        grad_scores, queries, (((0,), (0,)), ((), ())), preferred_element_type=jnp.float32
    ).astype(jnp.bfloat16)
    return (grad_queries, grad_keys, grad_values)


def cluster_grads(payload, validity, head_width):
    row_count = payload.shape[0]
    spans = payload.shape[1] // 4
    heads_local = spans // head_width
    positions = lax.broadcasted_iota(jnp.int32, (row_count, row_count), 0)
    others = lax.broadcasted_iota(jnp.int32, (row_count, row_count), 1)
    allowed = (positions >= others) & (validity[None, :] > 0)
    factor = head_width ** (-0.5)

    def one_head(head_index, result):
        offset = head_index * head_width

        def select(portion):
            return lax.dynamic_slice_in_dim(payload, portion * spans + offset, head_width, 1)

        grads_head = attend_backward(select(0), select(1), select(2), select(3), allowed, factor)
        for portion in range(3):
            result = lax.dynamic_update_slice_in_dim(
                result, grads_head[portion], portion * spans + offset, 1
            )
        return result

    return lax.fori_loop(0, heads_local, one_head, jnp.zeros((row_count, 3 * spans), jnp.bfloat16))


def on_device(hidden, norm_gain, projection, upstream, cluster):
    seq_count = lax.axis_size("seq")
    tokens = hidden.shape[1]
    width_model = hidden.shape[2]
    spans = projection.shape[2]
    clusters_all = CLUS_DEV * seq_count
    slot_rows = 3 * tokens // clusters_all
    scaled, spread, normed = normalize(hidden[0], norm_gain)
    labels = cluster[0, :, 0]
    member = (labels[:, None] == jnp.arange(clusters_all, dtype=jnp.int32)[None, :]).astype(
        jnp.int32
    )
    ranks = jnp.sum(jnp.cumsum(member, 0) * member, 1) - 1
    target = labels * slot_rows + ranks
    projected = jnp.einsum(
        "td,kdh->tkh", normed, projection, preferred_element_type=jnp.float32
    ).astype(jnp.bfloat16)
    payload = jnp.concatenate([projected.reshape(tokens, 3 * spans), upstream[0]], 1)
    columns = payload.shape[1]
    outgoing = jnp.zeros((clusters_all * slot_rows, columns), jnp.bfloat16).at[target].set(payload)
    outgoing = outgoing.reshape(seq_count, CLUS_DEV, slot_rows, columns)
    present = jnp.zeros((clusters_all * slot_rows,), jnp.bfloat16).at[target].set(1.0)
    present = present.reshape(seq_count, CLUS_DEV, slot_rows)
    rows_in = lax.all_to_all(outgoing, "seq", split_axis=0, concat_axis=0, tiled=True)
    marks_in = lax.all_to_all(present, "seq", split_axis=0, concat_axis=0, tiled=True)
    sources = rows_in.shape[0]
    item_count = rows_in.shape[1]
    stacked = jnp.swapaxes(rows_in, 0, 1).reshape(item_count, sources * slot_rows, rows_in.shape[3])
    mark_rows = jnp.swapaxes(marks_in, 0, 1).reshape(item_count, sources * slot_rows)

    def per_item(entries):
        return cluster_grads(entries[0], entries[1].astype(jnp.float32), HDIM)

    results = lax.map(per_item, (stacked, mark_rows))
    results = jnp.einsum(
        "irkh,kdh->ird",
        results.reshape(item_count, sources * slot_rows, 3, spans),
        projection,
        preferred_element_type=jnp.float32,
    ).astype(jnp.bfloat16)
    width_out = results.shape[-1]
    results = results.reshape(item_count, sources, slot_rows, width_out)
    answer = jnp.swapaxes(results, 0, 1)
    returned = lax.all_to_all(answer, "seq", split_axis=0, concat_axis=0, tiled=True)
    restored = returned.reshape(clusters_all * slot_rows, width_model)[target]
    partial_value = restored.astype(jnp.float32)
    half_width = width_model // lax.axis_size("head")
    offset = lax.axis_index("head") * half_width
    own_scaled = lax.dynamic_slice_in_dim(scaled, offset, half_width, 1)
    own_gain = lax.dynamic_slice_in_dim(norm_gain, offset, half_width, 0)
    gradient = lax.psum_scatter(
        partial_value.astype(jnp.bfloat16), "head", scatter_dimension=1, tiled=True
    ).astype(jnp.float32)
    scaled_grad = gradient * own_gain
    first_sum, second_sum = lax.psum(
        (
            jnp.sum(scaled_grad, -1, keepdims=True),
            jnp.sum(scaled_grad * own_scaled, -1, keepdims=True),
        ),
        "head",
    )
    first_mean = first_sum / width_model
    second_mean = second_sum / width_model
    input_gradient = (spread * (scaled_grad - first_mean - own_scaled * second_mean)).astype(
        jnp.bfloat16
    )
    local_sum = jnp.sum(gradient * own_scaled, 0)
    gain_total = lax.psum(local_sum, ("seq", "dp"))
    gain_gradient = gain_total * (seq_count * lax.axis_size("dp") * tokens) ** (-0.5)
    return (input_gradient.reshape(1, tokens, half_width), gain_gradient)


MESH = pl.DeviceIdType.MESH
LANES = 128
ROW_BLOCK = 256
NT = (((1,), (1,)), ((), ()))
TN = (((0,), (0,)), ((), ()))


def dot(left, right, dims=(((1,), (0,)), ((), ()))):
    return lax.dot_general(left, right, dims, preferred_element_type=jnp.float32)


def fused(
    n_seq, n_head, n_dp, total_rows,
    hidden_ref, gain_ref, proj_hbm, up_ref, label_ref,
    grad_ref, gain_out_ref,
    w_ref, scaled_ref, snd, rcv, labels_in, onehot, weights, acc_v, acc_k, gsend, gback,
    part_out, part_in, gain_src, gain_dp, gain_mid, gain_seq,
    w_sem, f_send, f_recv, l_send, l_recv, b_send, b_recv, h_send, h_recv,
    d_send, d_recv, s_send, s_recv,
):
    me = lax.axis_index("seq")
    core = lax.axis_index("head")
    group = lax.axis_index("dp")
    tokens, width = hidden_ref.shape
    spans = up_ref.shape[1]
    length = n_seq * tokens
    half = width // n_head
    heads = LANES // HDIM
    factor = HDIM ** (-0.5)

    w_copies = [pltpu.make_async_copy(proj_hbm.at[p], w_ref.at[p], w_sem.at[p]) for p in range(3)]
    for copy in w_copies:
        copy.start()
    barrier = pltpu.get_barrier_semaphore()
    peers = [("seq", me, n_seq), ("head", core, n_head), ("dp", group, n_dp)]
    for axis, index, size in peers:
        for o in range(1, size):
            pl.semaphore_signal(
                barrier, inc=1, device_id={axis: lax.rem(index + o, size)}, device_id_type=MESH
            )

    def remote(src, dst, send, recv, axis, index):
        return pltpu.make_async_remote_copy(
            src_ref=src, dst_ref=dst, send_sem=send, recv_sem=recv,
            device_id={axis: index}, device_id_type=MESH,
        )

    def rows_of(index):
        return pl.ds(pl.multiple_of(index * tokens, 16), tokens)

    def lanes_of(index):
        return pl.ds(pl.multiple_of(index * LANES, LANES), LANES)

    my_rows = rows_of(me)
    forward, label_copies = {}, []
    for o in range(1, n_seq):
        j = lax.rem(me + o, n_seq)
        for kind in range(4):
            src = up_ref.at[:, lanes_of(j)] if kind == 0 else snd.at[kind - 1, j]
            forward[kind, o] = remote(
                src, rcv.at[kind, my_rows], f_send.at[kind, o - 1], f_recv.at[kind, o - 1], "seq", j
            )
        label_copies.append(
            remote(label_ref, labels_in.at[me], l_send.at[o - 1], l_recv.at[o - 1], "seq", j)
        )

    values = hidden_ref[...].astype(jnp.float32)
    center = values - jnp.mean(values, -1, keepdims=True)
    spread = lax.rsqrt(jnp.mean(center * center, -1, keepdims=True) + epsilon)
    scaled = center * spread
    scaled_ref[...] = scaled
    normed = (scaled * gain_ref[...]).astype(jnp.bfloat16)

    pl.semaphore_wait(barrier, n_seq + n_head + n_dp - 3)
    for copy in label_copies:
        copy.start()
    for o in range(1, n_seq):
        forward[0, o].start()
    rcv[0, my_rows, :] = up_ref[:, lanes_of(me)]
    labels_in[me] = label_ref[...]
    for p in range(3):
        w_copies[p].wait()
        made = dot(normed, w_ref[p]).astype(jnp.bfloat16)
        for j in range(n_seq):
            snd[p, j] = made[:, j * LANES : (j + 1) * LANES]
        for o in range(1, n_seq):
            forward[p + 1, o].start()
        rcv[p + 1, my_rows, :] = snd[p, me]

    for copy in label_copies:
        copy.wait_recv()
    labels = labels_in[0]
    for j in range(1, n_seq):
        labels = labels + labels_in[j]
    classes = lax.broadcasted_iota(jnp.int32, (onehot.shape[0], LANES), 0).astype(jnp.float32)
    for c in range(length // LANES):
        hit = classes == labels[c : c + 1, :]
        onehot[:, c * LANES : (c + 1) * LANES] = jnp.where(hit, 1.0, 0.0).astype(jnp.bfloat16)

    lane_head = lax.broadcasted_iota(jnp.int32, (1, LANES), 1) // HDIM
    head_masks = [jnp.where(lane_head == h, 1.0, 0.0).astype(jnp.bfloat16) for h in range(heads)]
    blocks = list(reversed(range(length // ROW_BLOCK)))

    def arrived(kind):
        for o in range(1, n_seq):
            forward[kind, o].wait_recv()

    def send_back(portion):
        copies = []
        for o in range(1, n_seq):
            j = lax.rem(me + o, n_seq)
            copy = remote(
                gsend.at[portion, rows_of(j)], gback.at[portion, :, lanes_of(me)],
                b_send.at[portion, o - 1], b_recv.at[portion, o - 1], "seq", j,
            )
            copy.start()
            copies.append(copy)
        gback[portion, :, lanes_of(me)] = gsend[portion, my_rows, :]
        return copies

    for kind in (0, 1, 2):
        arrived(kind)
    for block in blocks:
        first, reach = block * ROW_BLOCK, (block + 1) * ROW_BLOCK
        same = dot(onehot[:, first:reach], onehot[:, :reach], TN)
        row_at = lax.broadcasted_iota(jnp.int32, (ROW_BLOCK, reach), 0) + first
        col_at = lax.broadcasted_iota(jnp.int32, (ROW_BLOCK, reach), 1)
        allowed = (same > 0.5) & (row_at >= col_at)
        for h in range(heads):
            query = rcv[1, first:reach, :] * head_masks[h]
            scores = dot(query, rcv[2, :reach, :], NT) * factor
            scores = jnp.where(allowed, scores, masked)
            powers = jnp.exp(scores - jnp.max(scores, -1, keepdims=True))
            weight = powers * (1.0 / jnp.sum(powers, -1, keepdims=True))
            weights[h, first:reach, :reach] = weight
            term = dot(weight.astype(jnp.bfloat16), rcv[0, first:reach, :] * head_masks[h], TN)
            if block == blocks[0] and h == 0:
                acc_v[...] = term
            else:
                acc_v[:reach, :] += term
    gsend[2] = acc_v[...].astype(jnp.bfloat16)
    back = {2: send_back(2)}

    arrived(3)
    for block in blocks:
        first, reach = block * ROW_BLOCK, (block + 1) * ROW_BLOCK
        grad_query = None
        for h in range(heads):
            weight = weights[h, first:reach, :reach]
            cotangent = rcv[0, first:reach, :] * head_masks[h]
            output = dot(weight.astype(jnp.bfloat16), rcv[3, :reach, :])
            middle = jnp.sum(cotangent.astype(jnp.float32) * output, -1, keepdims=True)
            grad_weights = dot(cotangent, rcv[3, :reach, :], NT)
            grad_scores = (weight * (grad_weights - middle) * factor).astype(jnp.bfloat16)
            found = dot(grad_scores, rcv[2, :reach, :])
            grad_query = found if h == 0 else jnp.where(lane_head == h, found, grad_query)
            term = dot(grad_scores, rcv[1, first:reach, :] * head_masks[h], TN)
            if block == blocks[0] and h == 0:
                acc_k[...] = term
            else:
                acc_k[:reach, :] += term
        gsend[0, first:reach, :] = grad_query.astype(jnp.bfloat16)
    back[0] = send_back(0)
    gsend[1] = acc_k[...].astype(jnp.bfloat16)
    back[1] = send_back(1)

    for portion in (2, 0, 1):
        for copy in back[portion]:
            copy.wait_recv()
    exchanges = []
    for c in range(2):
        cut = slice(c * width // 2, (c + 1) * width // 2)
        partial = dot(gback[0], w_ref[0, cut, :], NT)
        for p in (1, 2):
            partial = partial + dot(gback[p], w_ref[p, cut, :], NT)
        part_out[c] = partial.astype(jnp.bfloat16)
        copy = remote(
            part_out.at[c], part_in.at[c], h_send.at[c], h_recv.at[c], "head", lax.rem(core + 1, n_head)
        )
        copy.start()
        exchanges.append(copy)

    gradients, first_sum, second_sum = [], 0.0, 0.0
    for c in range(2):
        cut = slice(c * width // 2, (c + 1) * width // 2)
        exchanges[c].wait_recv()
        gradient = part_out[c].astype(jnp.float32) + part_in[c].astype(jnp.float32)
        scaled_grad = gradient * gain_ref[:, cut]
        own_scaled = scaled_ref[:, cut]
        first_sum = first_sum + jnp.sum(scaled_grad, -1, keepdims=True)
        second_sum = second_sum + jnp.sum(scaled_grad * own_scaled, -1, keepdims=True)
    own_cut = pl.ds(pl.multiple_of(core * half, LANES), half)
    gradient = part_out[core].astype(jnp.float32) + part_in[core].astype(jnp.float32)
    own_scaled = scaled_ref[:, own_cut]
    local_sum = jnp.sum(gradient * own_scaled, 0, keepdims=True)
    gain_src[...] = jnp.zeros_like(gain_src)
    for c in range(half // LANES):
        gain_src[c : c + 1, :] = local_sum[:, c * LANES : (c + 1) * LANES]
    over_dp = []
    for o in range(1, n_dp):
        copy = remote(
            gain_src, gain_dp.at[group], d_send.at[o - 1], d_recv.at[o - 1],
            "dp", lax.rem(group + o, n_dp),
        )
        copy.start()
        over_dp.append(copy)
    gain_dp[group] = gain_src[...]
    scaled_grad = gradient * gain_ref[:, own_cut]
    first_mean = first_sum / width
    second_mean = second_sum / width
    again = hidden_ref[...].astype(jnp.float32)
    again = again - jnp.mean(again, -1, keepdims=True)
    spread = lax.rsqrt(jnp.mean(again * again, -1, keepdims=True) + epsilon)
    grad_ref[...] = (spread * (scaled_grad - first_mean - own_scaled * second_mean)).astype(
        jnp.bfloat16
    )
    for copy in over_dp:
        copy.wait_recv()
    total = gain_dp[0]
    for j in range(1, n_dp):
        total = total + gain_dp[j]
    gain_mid[...] = total
    over_seq = []
    for o in range(1, n_seq):
        copy = remote(
            gain_mid, gain_seq.at[me], s_send.at[o - 1], s_recv.at[o - 1],
            "seq", lax.rem(me + o, n_seq),
        )
        copy.start()
        over_seq.append(copy)
    gain_seq[me] = total
    for copies in (label_copies, forward.values(), *back.values(), exchanges, over_dp):
        for copy in copies:
            copy.wait_send()
    for copy in over_seq:
        copy.wait()
    total = gain_seq[0]
    for j in range(1, n_seq):
        total = total + gain_seq[j]
    gain_out_ref[...] = total * total_rows ** (-0.5)


def on_device_heads(hidden, norm_gain, projection, upstream, cluster):
    n_seq, n_head, n_dp = (lax.axis_size(a) for a in ("seq", "head", "dp"))
    tokens, width = hidden.shape[1:]
    spans = projection.shape[2]
    length = n_seq * tokens
    heads = LANES // HDIM
    half = width // n_head
    label_rows = -(-length // (8 * LANES)) * 8
    class_rows = -(-(CLUS_DEV * n_seq) // 16) * 16
    labels = lax.dynamic_update_slice(
        jnp.zeros((label_rows * LANES,), jnp.float32),
        cluster[0, :, 0].astype(jnp.float32),
        (lax.axis_index("seq") * tokens,),
    ).reshape(label_rows, LANES)
    gain_rows = -(-half // (8 * LANES)) * 8
    vmem = pl.BlockSpec(memory_space=pltpu.VMEM)
    dma = pltpu.SemaphoreType.DMA
    bf16, f32 = jnp.bfloat16, jnp.float32
    gradient, gain = pl.pallas_call(
        functools.partial(fused, n_seq, n_head, n_dp, n_seq * n_dp * tokens),
        out_shape=(
            jax.ShapeDtypeStruct((tokens, half), bf16),
            jax.ShapeDtypeStruct((gain_rows, LANES), f32),
        ),
        in_specs=[vmem, vmem, pl.BlockSpec(memory_space=pl.ANY), vmem, vmem],
        out_specs=(vmem, vmem),
        scratch_shapes=[
            pltpu.VMEM((3, width, spans), bf16),
            pltpu.VMEM((tokens, width), f32),
            pltpu.VMEM((3, n_seq, tokens, LANES), bf16),
            pltpu.VMEM((4, length, LANES), bf16),
            pltpu.VMEM((n_seq, label_rows, LANES), f32),
            pltpu.VMEM((class_rows, length), bf16),
            pltpu.VMEM((heads, length, length), f32),
            pltpu.VMEM((length, LANES), f32),
            pltpu.VMEM((length, LANES), f32),
            pltpu.VMEM((3, length, LANES), bf16),
            pltpu.VMEM((3, tokens, spans), bf16),
            pltpu.VMEM((2, tokens, width // 2), bf16),
            pltpu.VMEM((2, tokens, width // 2), bf16),
            pltpu.VMEM((gain_rows, LANES), f32),
            pltpu.VMEM((n_dp, gain_rows, LANES), f32),
            pltpu.VMEM((gain_rows, LANES), f32),
            pltpu.VMEM((n_seq, gain_rows, LANES), f32),
            dma((3,)),
            dma((4, n_seq - 1)),
            dma((4, n_seq - 1)),
            dma((n_seq - 1,)),
            dma((n_seq - 1,)),
            dma((3, n_seq - 1)),
            dma((3, n_seq - 1)),
            dma((2,)),
            dma((2,)),
            dma((n_dp - 1,)),
            dma((n_dp - 1,)),
            dma((n_seq - 1,)),
            dma((n_seq - 1,)),
        ],
        compiler_params=pltpu.CompilerParams(collective_id=0, has_side_effects=True),
    )(hidden[0], norm_gain[None, :], projection, upstream[0], labels)
    gain_gradient = gain[: half // LANES].reshape(half)
    return (gradient.reshape(1, tokens, half), gain_gradient)


def splits_by_heads(mesh, hidden, projection):
    n_seq, n_head, n_dp = (mesh.shape[a] for a in ("seq", "head", "dp"))
    spans = projection.shape[2] // n_head
    return (
        n_head == 2
        and n_dp > 1
        and n_seq > 1
        and spans == n_seq * LANES
        and hidden.shape[1] % ROW_BLOCK == 0
        and hidden.shape[1] <= 4 * ROW_BLOCK
    )


def solution(mesh):
    in_specs = (
        P("dp", "seq", None),
        P(),
        P(None, None, "head"),
        P("dp", "seq", "head"),
        P("dp", "seq", None),
    )
    out_specs = (P("dp", "seq", "head"), P("head"))

    def program(hidden, norm_gain, projection, upstream, cluster):
        body = on_device_heads if splits_by_heads(mesh, hidden, projection) else on_device
        return jax.shard_map(
            body, mesh=mesh, in_specs=in_specs, out_specs=out_specs, check_vma=False
        )(hidden, norm_gain, projection, upstream, cluster)

    return program
```

```python
import functools

import jax
import jax.numpy as jnp
from jax import lax
from jax.experimental import pallas as pl
from jax.experimental.pallas import tpu as pltpu
from jax.sharding import PartitionSpec as P

HDIM = 64
CLUS_DEV = 1


epsilon = 1e-05
masked = -1e30


def normalize(values, norm_gain):
    values = values.astype(jnp.float32)
    center = values - jnp.mean(values, -1, keepdims=True)
    spread = lax.rsqrt(jnp.mean(center * center, -1, keepdims=True) + epsilon)
    scaled = center * spread
    return (scaled, spread, (scaled * norm_gain).astype(jnp.bfloat16))


def attend_backward(queries, key_rows, values, upstream, allowed, factor):
    scores = (
        lax.dot_general(
            queries, key_rows, (((1,), (1,)), ((), ())), preferred_element_type=jnp.float32
        )
        * factor
    )
    scores = jnp.where(allowed, scores, masked)
    powers = jnp.exp(scores - jnp.max(scores, -1, keepdims=True))
    weights = powers / jnp.sum(powers, -1, keepdims=True)
    rounded = weights.astype(jnp.bfloat16)
    output = jnp.dot(rounded, values, preferred_element_type=jnp.float32)
    center_term = jnp.sum(upstream.astype(jnp.float32) * output, -1, keepdims=True)
    grad_values = lax.dot_general(
        rounded, upstream, (((0,), (0,)), ((), ())), preferred_element_type=jnp.float32
    ).astype(jnp.bfloat16)
    grad_weights = lax.dot_general(
        upstream, values, (((1,), (1,)), ((), ())), preferred_element_type=jnp.float32
    )
    grad_scores = (weights * (grad_weights - center_term) * factor).astype(jnp.bfloat16)
    grad_queries = jnp.dot(grad_scores, key_rows, preferred_element_type=jnp.float32).astype(
        jnp.bfloat16
    )
    grad_keys = lax.dot_general(
        grad_scores, queries, (((0,), (0,)), ((), ())), preferred_element_type=jnp.float32
    ).astype(jnp.bfloat16)
    return (grad_queries, grad_keys, grad_values)


def cluster_grads(payload, validity, head_width):
    row_count = payload.shape[0]
    spans = payload.shape[1] // 4
    heads_local = spans // head_width
    positions = lax.broadcasted_iota(jnp.int32, (row_count, row_count), 0)
    others = lax.broadcasted_iota(jnp.int32, (row_count, row_count), 1)
    allowed = (positions >= others) & (validity[None, :] > 0)
    factor = head_width ** (-0.5)

    def one_head(head_index, result):
        offset = head_index * head_width

        def select(portion):
            return lax.dynamic_slice_in_dim(payload, portion * spans + offset, head_width, 1)

        grads_head = attend_backward(select(0), select(1), select(2), select(3), allowed, factor)
        for portion in range(3):
            result = lax.dynamic_update_slice_in_dim(
                result, grads_head[portion], portion * spans + offset, 1
            )
        return result

    return lax.fori_loop(0, heads_local, one_head, jnp.zeros((row_count, 3 * spans), jnp.bfloat16))


def on_device(hidden, norm_gain, projection, upstream, cluster):
    seq_count = lax.axis_size("seq")
    tokens = hidden.shape[1]
    width_model = hidden.shape[2]
    spans = projection.shape[2]
    clusters_all = CLUS_DEV * seq_count
    slot_rows = 3 * tokens // clusters_all
    scaled, spread, normed = normalize(hidden[0], norm_gain)
    labels = cluster[0, :, 0]
    member = (labels[:, None] == jnp.arange(clusters_all, dtype=jnp.int32)[None, :]).astype(
        jnp.int32
    )
    ranks = jnp.sum(jnp.cumsum(member, 0) * member, 1) - 1
    target = labels * slot_rows + ranks
    projected = jnp.einsum(
        "td,kdh->tkh", normed, projection, preferred_element_type=jnp.float32
    ).astype(jnp.bfloat16)
    payload = jnp.concatenate([projected.reshape(tokens, 3 * spans), upstream[0]], 1)
    columns = payload.shape[1]
    outgoing = jnp.zeros((clusters_all * slot_rows, columns), jnp.bfloat16).at[target].set(payload)
    outgoing = outgoing.reshape(seq_count, CLUS_DEV, slot_rows, columns)
    present = jnp.zeros((clusters_all * slot_rows,), jnp.bfloat16).at[target].set(1.0)
    present = present.reshape(seq_count, CLUS_DEV, slot_rows)
    rows_in = lax.all_to_all(outgoing, "seq", split_axis=0, concat_axis=0, tiled=True)
    marks_in = lax.all_to_all(present, "seq", split_axis=0, concat_axis=0, tiled=True)
    sources = rows_in.shape[0]
    item_count = rows_in.shape[1]
    stacked = jnp.swapaxes(rows_in, 0, 1).reshape(item_count, sources * slot_rows, rows_in.shape[3])
    mark_rows = jnp.swapaxes(marks_in, 0, 1).reshape(item_count, sources * slot_rows)

    def per_item(entries):
        return cluster_grads(entries[0], entries[1].astype(jnp.float32), HDIM)

    results = lax.map(per_item, (stacked, mark_rows))
    results = jnp.einsum(
        "irkh,kdh->ird",
        results.reshape(item_count, sources * slot_rows, 3, spans),
        projection,
        preferred_element_type=jnp.float32,
    ).astype(jnp.bfloat16)
    width_out = results.shape[-1]
    results = results.reshape(item_count, sources, slot_rows, width_out)
    answer = jnp.swapaxes(results, 0, 1)
    returned = lax.all_to_all(answer, "seq", split_axis=0, concat_axis=0, tiled=True)
    restored = returned.reshape(clusters_all * slot_rows, width_model)[target]
    partial_value = restored.astype(jnp.float32)
    half_width = width_model // lax.axis_size("head")
    offset = lax.axis_index("head") * half_width
    own_scaled = lax.dynamic_slice_in_dim(scaled, offset, half_width, 1)
    own_gain = lax.dynamic_slice_in_dim(norm_gain, offset, half_width, 0)
    gradient = lax.psum_scatter(
        partial_value.astype(jnp.bfloat16), "head", scatter_dimension=1, tiled=True
    ).astype(jnp.float32)
    scaled_grad = gradient * own_gain
    first_sum, second_sum = lax.psum(
        (
            jnp.sum(scaled_grad, -1, keepdims=True),
            jnp.sum(scaled_grad * own_scaled, -1, keepdims=True),
        ),
        "head",
    )
    first_mean = first_sum / width_model
    second_mean = second_sum / width_model
    input_gradient = (spread * (scaled_grad - first_mean - own_scaled * second_mean)).astype(
        jnp.bfloat16
    )
    local_sum = jnp.sum(gradient * own_scaled, 0)
    gain_total = lax.psum(local_sum, ("seq", "dp"))
    gain_gradient = gain_total * (seq_count * lax.axis_size("dp") * tokens) ** (-0.5)
    return (input_gradient.reshape(1, tokens, half_width), gain_gradient)


MESH = pl.DeviceIdType.MESH
LANES = 128
ROW_BLOCK = 256
NT = (((1,), (1,)), ((), ()))
TN = (((0,), (0,)), ((), ()))


def dot(left, right, dims=(((1,), (0,)), ((), ()))):
    return lax.dot_general(left, right, dims, preferred_element_type=jnp.float32)


def fused(
    n_seq, n_head, n_dp, total_rows,
    hidden_ref, gain_ref, proj_hbm, up_ref, label_ref,
    grad_ref, gain_out_ref,
    w_ref, scaled_ref, snd, rcv, labels_in, onehot, weights, acc_v, acc_k, gsend, gback,
    part_out, part_in, spread_ref, gain_src, gain_seq, gain_mid, gain_all, gain_sum,
    w_sem, f_send, f_recv, l_send, l_recv, b_send, b_recv, h_send, h_recv,
    s_send, s_recv, d_send, d_recv,
):
    me = lax.axis_index("seq")
    core = lax.axis_index("head")
    group = lax.axis_index("dp")
    tokens, width = hidden_ref.shape
    spans = up_ref.shape[1]
    length = n_seq * tokens
    half = width // n_head
    heads = LANES // HDIM
    factor = HDIM ** (-0.5)

    w_copies = [pltpu.make_async_copy(proj_hbm.at[p], w_ref.at[p], w_sem.at[p]) for p in range(3)]
    for copy in w_copies:
        copy.start()
    barrier = pltpu.get_barrier_semaphore()
    along = [{"seq": lax.rem(me + o, n_seq)} for o in range(1, n_seq)]
    across = [
        {"dp": lax.rem(group + o // n_head, n_dp), "head": lax.rem(core + o % n_head, n_head)}
        for o in range(1, n_dp * n_head)
    ]
    for peer in along + across:
        pl.semaphore_signal(barrier, inc=1, device_id=peer, device_id_type=MESH)

    def remote(src, dst, send, recv, peer):
        return pltpu.make_async_remote_copy(
            src_ref=src, dst_ref=dst, send_sem=send, recv_sem=recv,
            device_id=peer, device_id_type=MESH,
        )

    def rows_of(index):
        return pl.ds(pl.multiple_of(index * tokens, 16), tokens)

    def lanes_of(index):
        return pl.ds(pl.multiple_of(index * LANES, LANES), LANES)

    my_rows = rows_of(me)
    forward, label_copies = {}, []
    for o in range(1, n_seq):
        j = lax.rem(me + o, n_seq)
        for kind in range(4):
            src = up_ref.at[:, lanes_of(j)] if kind == 0 else snd.at[kind - 1, j]
            forward[kind, o] = remote(
                src, rcv.at[kind, my_rows], f_send.at[kind, o - 1], f_recv.at[kind, o - 1], along[o - 1]
            )
        label_copies.append(
            remote(label_ref, labels_in.at[me], l_send.at[o - 1], l_recv.at[o - 1], along[o - 1])
        )

    pl.semaphore_wait(barrier, len(along) + len(across))
    for copy in label_copies:
        copy.start()
    for o in range(1, n_seq):
        forward[0, o].start()
    values = hidden_ref[...].astype(jnp.float32)
    center = values - jnp.mean(values, -1, keepdims=True)
    spread = lax.rsqrt(jnp.mean(center * center, -1, keepdims=True) + epsilon)
    scaled = center * spread
    scaled_ref[...] = scaled
    spread_ref[...] = jnp.broadcast_to(spread, spread_ref.shape)
    normed = (scaled * gain_ref[...]).astype(jnp.bfloat16)

    rcv[0, my_rows, :] = up_ref[:, lanes_of(me)]
    labels_in[me] = label_ref[...]
    for p in range(3):
        w_copies[p].wait()
        made = dot(normed, w_ref[p]).astype(jnp.bfloat16)
        for j in range(n_seq):
            snd[p, j] = made[:, j * LANES : (j + 1) * LANES]
        for o in range(1, n_seq):
            forward[p + 1, o].start()
        rcv[p + 1, my_rows, :] = snd[p, me]

    for copy in label_copies:
        copy.wait_recv()
    labels = labels_in[0]
    for j in range(1, n_seq):
        labels = labels + labels_in[j]
    classes = lax.broadcasted_iota(jnp.int32, (onehot.shape[0], LANES), 0).astype(jnp.float32)
    for c in range(length // LANES):
        hit = classes == labels[c : c + 1, :]
        onehot[:, c * LANES : (c + 1) * LANES] = jnp.where(hit, 1.0, 0.0).astype(jnp.bfloat16)

    lane_head = lax.broadcasted_iota(jnp.int32, (1, LANES), 1) // HDIM
    head_masks = [jnp.where(lane_head == h, 1.0, 0.0).astype(jnp.bfloat16) for h in range(heads)]
    blocks = list(reversed(range(length // ROW_BLOCK)))

    def arrived(kind):
        for o in range(1, n_seq):
            forward[kind, o].wait_recv()

    back = {}

    def send_back(portion, first, count):
        for o in range(1, n_seq):
            j = lax.rem(me + o, n_seq)
            place = (portion, first // (tokens // 2), o - 1)
            source = pl.ds(pl.multiple_of(j * tokens + first, 16), count)
            copy = remote(
                gsend.at[portion, source],
                gback.at[portion, first : first + count, lanes_of(me)],
                b_send.at[place], b_recv.at[place], along[o - 1],
            )
            copy.start()
            back.setdefault(place[:2], []).append(copy)

    def keep_own(portion):
        gback[portion, :, lanes_of(me)] = gsend[portion, my_rows, :]

    for kind in (0, 1, 2):
        arrived(kind)
    for block in blocks:
        first, reach = block * ROW_BLOCK, (block + 1) * ROW_BLOCK
        same = dot(onehot[:, first:reach], onehot[:, :reach], TN)
        row_at = lax.broadcasted_iota(jnp.int32, (ROW_BLOCK, reach), 0) + first
        col_at = lax.broadcasted_iota(jnp.int32, (ROW_BLOCK, reach), 1)
        allowed = (same > 0.5) & (row_at >= col_at)
        for h in range(heads):
            query = rcv[1, first:reach, :] * head_masks[h]
            scores = dot(query, rcv[2, :reach, :], NT) * factor
            scores = jnp.where(allowed, scores, masked)
            powers = jnp.exp(scores - jnp.max(scores, -1, keepdims=True))
            weight = powers * (1.0 / jnp.sum(powers, -1, keepdims=True))
            weights[h, first:reach, :reach] = weight
            term = dot(weight.astype(jnp.bfloat16), rcv[0, first:reach, :] * head_masks[h], TN)
            if block == blocks[0] and h == 0:
                acc_v[...] = term
            else:
                acc_v[:reach, :] += term
    gsend[2] = acc_v[...].astype(jnp.bfloat16)
    send_back(2, 0, tokens)
    keep_own(2)

    arrived(3)
    for block in blocks:
        first, reach = block * ROW_BLOCK, (block + 1) * ROW_BLOCK
        grad_query = None
        for h in range(heads):
            weight = weights[h, first:reach, :reach]
            cotangent = rcv[0, first:reach, :] * head_masks[h]
            output = dot(weight.astype(jnp.bfloat16), rcv[3, :reach, :])
            middle = jnp.sum(cotangent.astype(jnp.float32) * output, -1, keepdims=True)
            grad_weights = dot(cotangent, rcv[3, :reach, :], NT)
            grad_scores = (weight * (grad_weights - middle) * factor).astype(jnp.bfloat16)
            found = dot(grad_scores, rcv[2, :reach, :])
            grad_query = found if h == 0 else jnp.where(lane_head == h, found, grad_query)
            term = dot(grad_scores, rcv[1, first:reach, :] * head_masks[h], TN)
            if block == blocks[0] and h == 0:
                acc_k[...] = term
            else:
                acc_k[:reach, :] += term
        gsend[0, first:reach, :] = grad_query.astype(jnp.bfloat16)
    gsend[1] = acc_k[...].astype(jnp.bfloat16)
    part = tokens // 2
    for first in (0, part):
        for portion in (0, 1):
            send_back(portion, first, part)
    keep_own(0)
    keep_own(1)

    own_cut = pl.ds(pl.multiple_of(core * half, LANES), half)
    exchanges, sums = {}, [0.0] * n_head

    def make_partial(a):
        rows = slice(a * part, (a + 1) * part)
        for c in range(n_head):
            cut = slice(c * half, (c + 1) * half)
            partial = dot(gback[2, rows, :], w_ref[2, cut, :], NT)
            for p in (0, 1):
                partial = partial + dot(gback[p, rows, :], w_ref[p, cut, :], NT)
            rounded = partial.astype(jnp.bfloat16)
            part_out[a, c] = rounded
            exchanges[a, c] = remote(
                part_out.at[a, c], part_in.at[a, c], h_send.at[a, c], h_recv.at[a, c],
                {"head": lax.rem(core + 1, n_head)},
            )
            exchanges[a, c].start()
            sums[c] = sums[c] + jnp.sum(
                rounded.astype(jnp.float32) * scaled_ref[rows, cut], 0, keepdims=True
            )

    def finish(a):
        rows = slice(a * part, (a + 1) * part)
        first_sum, second_sum = 0.0, 0.0
        for c in range(n_head):
            cut = slice(c * half, (c + 1) * half)
            exchanges[a, c].wait_recv()
            gradient = part_out[a, c].astype(jnp.float32) + part_in[a, c].astype(jnp.float32)
            scaled_grad = gradient * gain_ref[:, cut]
            first_sum = first_sum + jnp.sum(scaled_grad, -1, keepdims=True)
            second_sum = second_sum + jnp.sum(scaled_grad * scaled_ref[rows, cut], -1, keepdims=True)
        gradient = part_out[a, core].astype(jnp.float32) + part_in[a, core].astype(jnp.float32)
        inner = gradient * gain_ref[:, own_cut] - first_sum / width
        inner = inner - scaled_ref[rows, own_cut] * (second_sum / width)
        grad_ref[rows, :] = (spread_ref[rows, :1] * inner).astype(jnp.bfloat16)

    for place in ((2, 0), (0, 0), (1, 0)):
        for copy in back[place]:
            copy.wait_recv()
    make_partial(0)
    finish(0)
    for place in ((0, 1), (1, 1)):
        for copy in back[place]:
            copy.wait_recv()
    make_partial(1)

    half_rows = half // LANES
    for c in range(n_head):
        for i in range(half_rows):
            at = c * half_rows + i
            gain_src[at : at + 1, :] = sums[c][:, i * LANES : (i + 1) * LANES]
    over_seq, over_rest = [], []
    for o, peer in enumerate(along):
        over_seq.append(remote(gain_src, gain_seq.at[me], s_send.at[o], s_recv.at[o], peer))
        over_seq[-1].start()
    gain_seq[me] = gain_src[...]
    finish(1)
    for copy in over_seq:
        copy.wait_recv()
    total = gain_seq[0]
    for j in range(1, n_seq):
        total = total + gain_seq[j]
    gain_mid[...] = total
    slot = group * n_head + core
    for o, peer in enumerate(across):
        over_rest.append(remote(gain_mid, gain_all.at[slot], d_send.at[o], d_recv.at[o], peer))
        over_rest[-1].start()
    gain_all[slot] = total
    for copies in (label_copies, forward.values(), *back.values(), exchanges.values(), over_seq):
        for copy in copies:
            copy.wait_send()
    for copy in over_rest:
        copy.wait()
    total = gain_all[0]
    for j in range(1, n_dp * n_head):
        total = total + gain_all[j]
    gain_sum[...] = total * total_rows ** (-0.5)
    for i in range(half_rows):
        gain_out_ref[:, i * LANES : (i + 1) * LANES] = gain_sum[pl.ds(core * half_rows + i, 1), :]


def on_device_heads(hidden, norm_gain, projection, upstream, cluster):
    n_seq, n_head, n_dp = (lax.axis_size(a) for a in ("seq", "head", "dp"))
    tokens, width = hidden.shape[1:]
    spans = projection.shape[2]
    length = n_seq * tokens
    heads = LANES // HDIM
    half = width // n_head
    label_rows = -(-length // (8 * LANES)) * 8
    class_rows = -(-(CLUS_DEV * n_seq) // 16) * 16
    labels = lax.dynamic_update_slice(
        jnp.zeros((label_rows * LANES,), jnp.float32),
        cluster[0, :, 0].astype(jnp.float32),
        (lax.axis_index("seq") * tokens,),
    ).reshape(label_rows, LANES)
    gain_rows = width // LANES
    vmem = pl.BlockSpec(memory_space=pltpu.VMEM)
    dma = pltpu.SemaphoreType.DMA
    bf16, f32 = jnp.bfloat16, jnp.float32
    gradient, gain = pl.pallas_call(
        functools.partial(fused, n_seq, n_head, n_dp, n_seq * n_dp * tokens),
        out_shape=(
            jax.ShapeDtypeStruct((tokens, half), bf16),
            jax.ShapeDtypeStruct((1, half), f32),
        ),
        in_specs=[vmem, vmem, pl.BlockSpec(memory_space=pl.ANY), vmem, vmem],
        out_specs=(vmem, vmem),
        scratch_shapes=[
            pltpu.VMEM((3, width, spans), bf16),
            pltpu.VMEM((tokens, width), f32),
            pltpu.VMEM((3, n_seq, tokens, LANES), bf16),
            pltpu.VMEM((4, length, LANES), bf16),
            pltpu.VMEM((n_seq, label_rows, LANES), f32),
            pltpu.VMEM((class_rows, length), bf16),
            pltpu.VMEM((heads, length, length), f32),
            pltpu.VMEM((length, LANES), f32),
            pltpu.VMEM((length, LANES), f32),
            pltpu.VMEM((3, length, LANES), bf16),
            pltpu.VMEM((3, tokens, spans), bf16),
            pltpu.VMEM((2, n_head, tokens // 2, half), bf16),
            pltpu.VMEM((2, n_head, tokens // 2, half), bf16),
            pltpu.VMEM((tokens, LANES), f32),
            pltpu.VMEM((gain_rows, LANES), f32),
            pltpu.VMEM((n_seq, gain_rows, LANES), f32),
            pltpu.VMEM((gain_rows, LANES), f32),
            pltpu.VMEM((n_dp * n_head, gain_rows, LANES), f32),
            pltpu.VMEM((gain_rows, LANES), f32),
            dma((3,)),
            dma((4, n_seq - 1)),
            dma((4, n_seq - 1)),
            dma((n_seq - 1,)),
            dma((n_seq - 1,)),
            dma((3, 2, n_seq - 1)),
            dma((3, 2, n_seq - 1)),
            dma((2, n_head)),
            dma((2, n_head)),
            dma((n_seq - 1,)),
            dma((n_seq - 1,)),
            dma((n_dp * n_head - 1,)),
            dma((n_dp * n_head - 1,)),
        ],
        compiler_params=pltpu.CompilerParams(collective_id=0, has_side_effects=True),
    )(hidden[0], norm_gain[None, :], projection, upstream[0], labels)
    return (gradient.reshape(1, tokens, half), gain.reshape(half))


def splits_by_heads(mesh, hidden, projection):
    n_seq, n_head, n_dp = (mesh.shape[a] for a in ("seq", "head", "dp"))
    spans = projection.shape[2] // n_head
    return (
        n_head == 2
        and n_dp > 1
        and n_seq > 1
        and spans == n_seq * LANES
        and hidden.shape[1] % ROW_BLOCK == 0
        and hidden.shape[1] <= 4 * ROW_BLOCK
    )


def solution(mesh):
    in_specs = (
        P("dp", "seq", None),
        P(),
        P(None, None, "head"),
        P("dp", "seq", "head"),
        P("dp", "seq", None),
    )
    out_specs = (P("dp", "seq", "head"), P("head"))

    def program(hidden, norm_gain, projection, upstream, cluster):
        body = on_device_heads if splits_by_heads(mesh, hidden, projection) else on_device
        return jax.shard_map(
            body, mesh=mesh, in_specs=in_specs, out_specs=out_specs, check_vma=False
        )(hidden, norm_gain, projection, upstream, cluster)

    return program
```
